32 devices in a mesh: comp: 16 (over z, y, core), io: 2 (over x).
Axes of the slice: x: 2, y: 2, z: 4, core: 2. Of those that a mesh axis runs over, the one named last changes fastest.
Arguments:
- tracer: float32 [40, 32, 2048], P(None, 'io', 'comp'), may hold values from -6 to 6
- anchor: float32 [40, 32, 2048], P(None, 'io', 'comp'), may hold values from -6 to 6
- east_flow: float32 [40, 32, 2048], P(None, 'io', 'comp'), may hold values from -0.15 to 0.15
- north_flow: float32 [40, 32, 2048], P(None, 'io', 'comp'), may hold values from -0.15 to 0.15
- diffusivity: float32 [40, 32, 2048], P(None, 'io', 'comp'), may hold values from 0.01 to 0.08
- land_mask: int32 [32, 2048], P('io', 'comp'), may hold values from 0 to 1, as said below
- block_dest: int32 [16, 32, 1], P('comp', 'io'), may hold values from 0 to 1; in each aligned block of 16 rows (0 to 15, 16 to 31, ..., all dimensions but the last counted through in order) at most 12 rows name the same one
Outputs:
- tracer_out: float32 [40, 32, 2048], P(None, 'io', 'comp')
- restart: float32 [4, 12, 40, 2048], P('io', None, None, 'comp')
- partner_copy: float32 [4, 12, 40, 2048], P('io', None, None, 'comp')
The draws below stay inside these ranges and needn't reach their ends.
Inputs may be any that keep to these rules, and one draw needn't show every extreme that they name: `land_mask`: the first and the last of the 32 rows are land. `block_dest`: among the 16 blocks of one tile no aggregator is named more than 12 times.
All inputs are finite; a program needn't handle non-finite values.
Results may differ from the reference program's by a relative error of at most 0.0003.
Values sent between devices are 32-bit elements; how exact they have to be, the bound alone decides.
A program may use at most 64 MiB of HBM per device.

```python
import math
import jax
import jax.numpy as jnp
import numpy as np
from jax import lax

LEV = 40
CLAT = 16
CLON = 128
BLK = 128
NBLK = 16
CAPB = 12
NLAT = 32
NLON = 2048
N_COMP = 16
N_IO = 2


def draw_land_mask(key, part):
    first_key, second_key = jax.random.split(jax.random.fold_in(key, 11))
    tile_level = jax.random.randint(first_key, (N_IO, 1, N_COMP, 1), 0, 8)
    cell_level = jax.random.randint(second_key, (N_IO, CLAT, N_COMP, CLON), 0, 16)
    ocean = (cell_level >= tile_level).astype(jnp.int32).reshape(NLAT, NLON)
    row_index = jnp.arange(NLAT, dtype=jnp.int32)[:, None]
    inside = ((row_index > 0) & (row_index < NLAT - 1)).astype(jnp.int32)
    return ocean * inside


def steps_of(stream_key, shape, cuts, least, high):
    def one(axis_at, parts):
        heights = jax.random.uniform(jax.random.fold_in(jax.random.fold_in(stream_key, 6), axis_at), (parts,), jnp.float32, least / len(cuts), high / len(cuts))
        return jnp.repeat(jnp.exp(heights), shape[axis_at] // parts).reshape((-1,) + (1,) * (len(shape) - axis_at - 1))

    level = one(*cuts[0])
    for cut in cuts[1:]:
        level = level * one(*cut)
    return level


def shared_out(key, own, number, rows, amount, top, most, skew):
    order = jax.random.permutation(key, amount)
    heavy_load, ordinary = shares(amount, rows * top, most, skew, True), shares(amount, rows * top, most, skew, False)
    places = jnp.arange(amount)

    def named(tallies, turn):
        used = int((tallies > 0).sum())
        fixed = max(1, used // 4)
        shifted = fixed + (places - fixed + turn * (used - fixed)) % max(1, amount - fixed)
        return jnp.zeros((amount,), jnp.int32).at[order[jnp.where(places < fixed, places, shifted)]].set(jnp.asarray(tallies, jnp.int32))

    tallies = jnp.where(number % 4 == 0, named(heavy_load, number // 4), named(ordinary, number - number // 4 - 1))
    mixed = jax.random.permutation(jax.random.fold_in(own, 3), amount)
    donor, receiver = mixed[0:amount // 2 * 2:2], mixed[1:amount // 2 * 2:2]
    slack = jnp.minimum(tallies[donor] - 1, most - tallies[receiver]) // 2
    slack = jnp.where((donor == order[0]) | (receiver == order[0]) | (tallies[receiver] == 0), 0, jnp.maximum(slack, 0))
    shifted = jax.random.randint(jax.random.fold_in(own, 4), (amount // 2,), 0, 1 << 20) % (slack + 1)
    tallies = tallies.at[donor].add(-shifted).at[receiver].add(shifted)
    items = jnp.searchsorted(jnp.cumsum(tallies), jnp.arange(rows * top), side="right").astype(jnp.int32)
    table = items.reshape(top, rows).T
    table = table[jax.random.permutation(jax.random.fold_in(own, 1), rows)]
    turn = jax.random.randint(jax.random.fold_in(own, 2), (rows, 1), 0, top)
    return jnp.take_along_axis(table, (jnp.arange(top)[None, :] + turn) % top, axis=1)


def shares(number_of, total, most, lean, full):
    weights = [(1 << 20) // math.isqrt(grade ** lean) + 1 for grade in range(1, number_of + 1)]
    largest = most if full else min(most, max(-(-total // number_of), total * weights[0] // sum(weights)))
    least = 1 if total - largest >= number_of - 1 else 0
    counts, spare = [largest] + [least] * (number_of - 1), total - largest - least * (number_of - 1)
    while spare > 0:
        movable = [i for i in range(1, number_of) if counts[i] < largest] or [i for i in range(1, number_of) if counts[i] < most]
        pool, left = sum([weights[i] for i in movable]), spare
        for i in movable:
            addition = min(most - counts[i], max(1, left * weights[i] // pool), spare)
            counts[i] = counts[i] + addition
            spare = spare - addition
    return np.array(counts)


def centred(stream_key, extent, deviation, bound, shards=(), kind=jnp.bfloat16):
    values = jax.random.normal(stream_key, extent, jnp.float32) * deviation
    if len(shards) > 0:
        values = steps_of(stream_key, extent, shards, -0.22, 0.18) * values
    return jnp.clip(values, min=-bound, max=bound).astype(kind)


def setup_inputs(seed: int = 0) -> dict:
    arg_keys = jax.random.split(jax.random.key(seed), 8)
    tracer = centred(arg_keys[0], (LEV, NLAT, NLON), 1.0, 6.0, ((1, 2), (2, 16)), jnp.float32)
    anchor = centred(arg_keys[1], (LEV, NLAT, NLON), 1.0, 6.0, ((1, 2), (2, 16)), jnp.float32)
    east_flow = jnp.clip(jax.random.uniform(arg_keys[2], (LEV, NLAT, NLON), jnp.float32, -0.15, 0.15) * steps_of(arg_keys[2], (LEV, NLAT, NLON), ((1, 2), (2, 16)), -0.4, 0.0), -0.15, 0.15)
    north_flow = jnp.clip(jax.random.uniform(arg_keys[3], (LEV, NLAT, NLON), jnp.float32, -0.15, 0.15) * steps_of(arg_keys[3], (LEV, NLAT, NLON), ((1, 2), (2, 16)), -0.4, 0.0), -0.15, 0.15)
    diffusivity = jnp.clip(jnp.exp(math.log(0.08) - 2.0794415 * jax.random.uniform(arg_keys[4], (LEV, NLAT, NLON), jnp.float32) ** steps_of(arg_keys[4], (LEV, NLAT, NLON), ((1, 2), (2, 16)), -0.2, 0.2)), 0.01, 0.08)
    land_mask = draw_land_mask(jax.random.fold_in(arg_keys[7], 71), 0)
    block_dest_keys = jax.random.split(jax.random.fold_in(arg_keys[6], 1), N_COMP * (N_IO * NBLK) // NBLK)
    block_dest_turns = jax.random.permutation(jax.random.fold_in(arg_keys[6], 3), N_COMP * (N_IO * NBLK) // NBLK)
    block_dest = jax.vmap(lambda own, number: shared_out(jax.random.fold_in(arg_keys[6], 2), own, number, NBLK, N_IO, 1, CAPB, 2))(block_dest_keys, block_dest_turns).reshape((N_COMP, N_IO * NBLK, 1))
    return dict(tracer=tracer, anchor=anchor, east_flow=east_flow, north_flow=north_flow, diffusivity=diffusivity, land_mask=land_mask, block_dest=block_dest)


def advance(field, east_flow, north_flow, diffusivity, east_open, north_open):
    field_e = jnp.roll(field, -1, axis=2)
    field_n = jnp.roll(field, -1, axis=1)
    flux_east = east_open * (jnp.maximum(east_flow, 0.0) * field + jnp.minimum(east_flow, 0.0) * field_e - diffusivity * (field_e - field))
    flux_north = north_open * (jnp.maximum(north_flow, 0.0) * field + jnp.minimum(north_flow, 0.0) * field_n - diffusivity * (field_n - field))
    return field - (flux_east - jnp.roll(flux_east, 1, axis=2)) - (flux_north - jnp.roll(flux_north, 1, axis=1))


def pack_tile(delta_tile, mask_tile, dest):
    total = mask_tile.shape[0]
    places = jnp.cumsum(mask_tile, dtype=jnp.int32) - 1
    target = jnp.where(mask_tile == 1, places, total).astype(jnp.int32)
    packed = jnp.zeros((LEV, total + 1), delta_tile.dtype).at[:, target].set(delta_tile)[:, :total]
    blocks = packed.reshape(LEV, NBLK, BLK)
    onehot = (dest[:, None] == jnp.arange(N_IO, dtype=jnp.int32)[None, :]).astype(jnp.int32)
    earlier = jnp.cumsum(onehot, axis=0, dtype=jnp.int32) - onehot
    ranks = jnp.sum(earlier * onehot, axis=1, dtype=jnp.int32)
    slots = dest * CAPB + ranks
    select = (jnp.arange(N_IO * CAPB, dtype=jnp.int32)[:, None] == slots[None, :]).astype(delta_tile.dtype)
    sendbuf = jnp.einsum("qk,lkb->qlb", select, blocks, precision=lax.Precision.HIGHEST)
    return sendbuf.reshape(N_IO, CAPB, LEV, BLK)


def reference(tracer, anchor, east_flow, north_flow, diffusivity, land_mask, block_dest):
    ocean = land_mask.astype(tracer.dtype)
    east_open = ocean * jnp.roll(ocean, -1, axis=1)
    north_open = ocean * jnp.roll(ocean, -1, axis=0)
    field = tracer
    for step in range(2):
        field = advance(field, east_flow, north_flow, diffusivity, east_open, north_open)
    delta = field - anchor
    tiles = delta.reshape(LEV, N_IO, CLAT, N_COMP, CLON).transpose(3, 1, 0, 2, 4).reshape(N_COMP * N_IO, LEV, CLAT * CLON)
    masks = land_mask.reshape(N_IO, CLAT, N_COMP, CLON).transpose(2, 0, 1, 3).reshape(N_COMP * N_IO, CLAT * CLON)
    dests = block_dest.reshape(N_COMP * N_IO, NBLK)
    sends = jax.vmap(pack_tile)(tiles, masks, dests)
    sends = sends.reshape(N_COMP, N_IO, N_IO, CAPB, LEV, BLK)
    restart = sends.transpose(2, 1, 3, 4, 0, 5).reshape(N_IO * N_IO, CAPB, LEV, N_COMP * BLK)
    shaped = restart.reshape(N_IO * N_IO, CAPB, LEV, N_COMP, BLK)
    partner_copy = jnp.roll(shaped, N_COMP // 2, axis=3).reshape(N_IO * N_IO, CAPB, LEV, N_COMP * BLK)
    return field, restart, partner_copy
```

```python
import functools
import jax
import jax.numpy as jnp
from jax import lax
from jax.experimental import pallas as pl
from jax.experimental.pallas import tpu as pltpu
from jax.sharding import PartitionSpec as P

MESH = pl.DeviceIdType.MESH
F32 = jnp.float32
BF16 = jnp.bfloat16


def kernel(cap, chunks, tracer, anchor, eflow, nflow, diff, mask, dest,
           out, restart, partner,
           f0, anc, ae, an, dd, be, bn, f1, mi, mf,
           east_s, west_s, east_r, west_r, north_s, south_s, north_r, south_r,
           packed, slots, slots2, table_v, table_p, table_s, table_ps,
           load_sem, table_sem, hs, hr, ps, pr, xs, xr, ys, yr, *got):
    n_comp, n_io = lax.axis_size("comp"), lax.axis_size("io")
    c, a = lax.axis_index("comp"), lax.axis_index("io")
    levels, rows, cols = tracer.shape
    east, west = lax.rem(c + 1, n_comp), lax.rem(c + n_comp - 1, n_comp)
    mate = lax.rem(c + n_comp // 2, n_comp)
    has_north, has_south = a < n_io - 1, a > 0

    zero = jnp.zeros((levels, cols), F32)
    for ref in (north_r, south_r):
        for k in range(3):
            ref[k] = zero

    barrier = pltpu.get_barrier_semaphore()
    for other in (east, west, mate):
        pl.semaphore_signal(barrier, inc=1, device_id={"comp": other}, device_id_type=MESH)
    for t in range(1, n_io):
        pl.semaphore_signal(barrier, inc=1, device_id={"io": lax.rem(a + t, n_io)}, device_id_type=MESH)

    loads = []
    mask_load = pltpu.make_async_copy(mask, mi, load_sem.at[5, 0])
    mask_load.start()
    for k, (src, dst) in enumerate(((tracer, f0), (eflow, ae), (nflow, an), (diff, dd), (anchor, anc))):
        for r in range(rows):
            cp = pltpu.make_async_copy(src.at[:, r, :], dst.at[r], load_sem.at[k, r])
            cp.start()
            loads.append(cp)

    lane = lax.broadcasted_iota(jnp.int32, (levels, cols), 1)
    packed[rows] = zero
    for ref in got:
        ref[rows] = zero[:levels // chunks]

    mask_load.wait()
    mf[...] = mi[...].astype(F32)
    m = mf[...]
    mb = m.astype(BF16)
    qi = lax.broadcasted_iota(jnp.int32, (cols, cols), 0)
    qj = lax.broadcasted_iota(jnp.int32, (cols, cols), 1)
    ki = lax.broadcasted_iota(jnp.int32, (rows, rows), 0)
    kj = lax.broadcasted_iota(jnp.int32, (rows, rows), 1)
    upto = jnp.where(qi <= qj, 1.0, 0.0).astype(BF16)
    before = jnp.where(kj < ki, 1.0, 0.0).astype(BF16)
    cum = jnp.dot(mb, upto, preferred_element_type=F32)
    tot = jnp.dot(mb, jnp.ones((cols, cols), BF16), preferred_element_type=F32)
    start = jnp.dot(before, tot.astype(BF16), preferred_element_type=F32)
    place = (start + cum - 1.0).astype(jnp.int32)
    place = jnp.where(m > 0.5, place & (cols - 1), -1)
    full_before = jnp.maximum(jnp.ceil(start * (1.0 / cols)) - 1.0, 0.0)
    full_after = jnp.maximum(jnp.ceil((start + tot) * (1.0 / cols)) - 1.0, 0.0)
    fill = start - full_before * cols
    over = full_after > full_before
    kk = lax.broadcasted_iota(jnp.int32, (rows, cols), 0)
    qq = lax.broadcasted_iota(jnp.int32, (rows, cols), 1)
    dvec = jnp.zeros((rows, cols), jnp.int32)
    for k in range(rows):
        dvec = jnp.where(kk == k, dest[k], dvec)
    group = jnp.zeros((rows, cols), jnp.int32)
    for g in range(1, n_io + 1):
        group = group + jnp.where(qq >= g * cap, 1, 0)
    slot = qq - group * cap
    hit = jnp.where(dvec == group, 1.0, 0.0)
    earlier = jnp.dot(before, hit.astype(BF16), preferred_element_type=F32)
    chosen = (dvec == group) & (earlier == slot.astype(F32))
    kq = jnp.min(jnp.where(chosen, kk, 1000).astype(F32), axis=0, keepdims=True)
    where_at = jnp.sum(jnp.where(full_after <= kq, 1.0, 0.0), axis=0, keepdims=True) - 1.0
    where_at = where_at + jnp.where(kq > full_after[rows - 1:rows], 1.0, 0.0)
    table_v[...] = jnp.broadcast_to(where_at.astype(jnp.int32), table_v.shape)
    table_load = pltpu.make_async_copy(table_v, table_s, table_sem.at[0])
    table_load.start()

    for cp in loads[:4 * rows]:
        cp.wait()

    for r in range(rows):
        mr = m[r:r + 1]
        u, v, d = ae[r], an[r], dd[r]
        ae[r] = mr * (jnp.maximum(u, 0.0) + d)
        be[r] = mr * (jnp.minimum(u, 0.0) - d)
        an[r] = mr * (jnp.maximum(v, 0.0) + d)
        bn[r] = mr * (jnp.minimum(v, 0.0) - d)

    last = cols - 1
    acc_e, acc_w = zero, zero
    for r in range(rows):
        acc_e = jnp.where(lane == r, (ae[r] * f0[r])[:, last:], acc_e)
        acc_e = jnp.where(lane == rows + r, be[r][:, last:], acc_e)
        acc_w = jnp.where(lane == r, f0[r][:, :1], acc_w)
        acc_w = jnp.where(lane == rows + r, jnp.broadcast_to(m[r:r + 1, :1], (levels, 1)), acc_w)
    east_s[0] = acc_e
    west_s[0] = acc_w
    north_s[0] = an[rows - 1] * f0[rows - 1]
    north_s[1] = bn[rows - 1]
    south_s[0] = f0[0]
    south_s[1] = jnp.broadcast_to(m[0:1], (levels, cols))

    pl.semaphore_wait(barrier, 3 + n_io - 1)

    def halo(step):
        where = slice(0, 2) if step == 0 else slice(2, 3)
        sel = pl.ds(where.start, where.stop - where.start)
        moves = [
            pltpu.make_async_remote_copy(east_s.at[step], east_r.at[step], hs.at[step, 0], hr.at[step, 0],
                                         device_id={"comp": east}, device_id_type=MESH),
            pltpu.make_async_remote_copy(west_s.at[step], west_r.at[step], hs.at[step, 1], hr.at[step, 1],
                                         device_id={"comp": west}, device_id_type=MESH),
        ]
        up = pltpu.make_async_remote_copy(north_s.at[sel], north_r.at[sel], hs.at[step, 2], hr.at[step, 2],
                                          device_id={"io": jnp.minimum(a + 1, n_io - 1)}, device_id_type=MESH)
        down = pltpu.make_async_remote_copy(south_s.at[sel], south_r.at[sel], hs.at[step, 3], hr.at[step, 3],
                                            device_id={"io": jnp.maximum(a - 1, 0)}, device_id_type=MESH)
        return moves, up, down

    def send_halo(step):
        moves, up, down = halo(step)
        for mv in moves:
            mv.start()
        pl.when(has_north)(up.start)
        pl.when(has_south)(down.start)

    def wait_halo(step):
        moves, up, down = halo(step)
        for mv in moves:
            mv.wait()

        @pl.when(has_north)
        def _():
            up.wait_send()
            down.wait_recv()

        @pl.when(has_south)
        def _():
            down.wait_send()
            up.wait_recv()

    send_halo(0)
    table_move = pltpu.make_async_remote_copy(table_v, table_p, ps.at[chunks], pr.at[chunks],
                                              device_id={"comp": mate}, device_id_type=MESH)
    table_move.start()
    wait_halo(0)

    west_0 = west_r[0]
    for r in range(rows):
        me = jnp.where(lane == last, west_0[:, rows + r:rows + r + 1], pltpu.roll(jnp.broadcast_to(m[r:r + 1], (levels, cols)), last, 1))
        ae[r] = ae[r] * me
        be[r] = be[r] * me
        mn = m[r + 1:r + 2] if r < rows - 1 else south_r[1]
        an[r] = an[r] * mn
        bn[r] = bn[r] * mn

    def row_of(step, src, r, fn_below):
        f = src[r]
        e_r, w_r = east_r[step], west_r[step]
        fe = jnp.where(lane == last, w_r[:, r:r + 1], pltpu.roll(f, last, 1))
        flux = ae[r] * f + be[r] * fe
        edge = m[r:r + 1] * (e_r[:, r:r + 1] + east_r[0][:, rows + r:rows + r + 1] * f)
        flux_w = jnp.where(lane == 0, edge, pltpu.roll(flux, 1, 1))
        fn = src[r + 1] if r < rows - 1 else south_r[0 if step == 0 else 2]
        flux_n = an[r] * f + bn[r] * fn
        return f - (flux - flux_w) - (flux_n - fn_below), flux_n

    flux_n = m[0:1] * (north_r[0] + north_r[1] * f0[0])
    acc_e, acc_w = zero, zero
    for r in range(rows):
        new, flux_n = row_of(0, f0, r, flux_n)
        f1[r] = new
        acc_e = jnp.where(lane == r, (ae[r] * new)[:, last:], acc_e)
        acc_w = jnp.where(lane == r, new[:, :1], acc_w)
        if r == 0:
            south_s[2] = new
        if r == rows - 1:
            north_s[2] = an[r] * new
    east_s[1] = acc_e
    west_s[1] = acc_w
    send_halo(1)
    for cp in loads[4 * rows:]:
        cp.wait()
    wait_halo(1)

    flux_n = m[0:1] * (north_r[2] + north_r[1] * f1[0])
    sub = lax.broadcasted_iota(jnp.int32, (cols, cols), 0)
    acc = zero
    outs = []
    for r in range(rows):
        new, flux_n = row_of(1, f1, r, flux_n)
        f0[r] = new
        delta = new - anc[r]
        hi = delta.astype(BF16).astype(F32)
        mid = (delta - hi).astype(BF16).astype(F32)
        low = delta - hi - mid
        parts = jnp.concatenate([hi, mid, low], axis=0).astype(BF16)
        pick = jnp.where(sub == place[r:r + 1], 1.0, 0.0).astype(BF16)
        got_r = lax.dot_general(parts, pick, (((1,), (1,)), ((), ())), preferred_element_type=F32)
        row = got_r[:levels] + got_r[levels:2 * levels] + got_r[2 * levels:]
        lanef = lane.astype(F32)
        begins = fill[r:r + 1]
        now = acc + jnp.where(lanef >= begins, row, 0.0)
        if r > 0:
            packed[r - 1] = now
        crossed = jnp.broadcast_to(jnp.where(over[r:r + 1], 1.0, 0.0), (levels, cols)) > 0.5
        acc = jnp.where(crossed, jnp.where(lanef < begins, row, 0.0), now)
    packed[rows - 1] = acc

    for r in range(rows):
        cp = pltpu.make_async_copy(f0.at[r], out.at[:, r, :], load_sem.at[0, r])
        cp.start()
        outs.append(cp)

    step_l = levels // chunks
    to_mate = []
    for k in range(chunks):
        part = pl.ds(k * step_l, step_l)
        cp = pltpu.make_async_remote_copy(packed.at[pl.ds(0, rows), part], got[k].at[pl.ds(0, rows)], ps.at[k], pr.at[k],
                                          device_id={"comp": mate}, device_id_type=MESH)
        cp.start()
        to_mate.append(cp)

    table_load.wait()
    pending = []
    for t in range(1, n_io):
        g = lax.rem(a + t, n_io)
        for s in range(cap):
            slots[t - 1, s] = packed[jnp.clip(table_s[0, g * cap + s], 0, rows)]
        cp = pltpu.make_async_remote_copy(slots.at[t - 1], restart.at[a], xs.at[t], xr.at[t],
                                          device_id={"io": g}, device_id_type=MESH)
        cp.start()
        pending.append(cp)
    for s in range(cap):
        restart[a, s] = packed[jnp.clip(table_s[0, a * cap + s], 0, rows)]

    table_move.wait()
    table_load = pltpu.make_async_copy(table_p, table_ps, table_sem.at[1])
    table_load.start()
    table_load.wait()
    for k in range(chunks):
        part = pl.ds(k * step_l, step_l)
        to_mate[k].wait_recv()
        for t in range(1, n_io):
            g = lax.rem(a + t, n_io)
            for s in range(cap):
                slots2[t - 1, s, part] = got[k][jnp.clip(table_ps[0, g * cap + s], 0, rows)]
            cp = pltpu.make_async_remote_copy(slots2.at[t - 1, :, part], partner.at[a, :, part], ys.at[t, k], yr.at[t, k],
                                              device_id={"io": g}, device_id_type=MESH)
            cp.start()
            pending.append(cp)
        for s in range(cap):
            partner[a, s, part] = got[k][jnp.clip(table_ps[0, a * cap + s], 0, rows)]
    for cp in to_mate:
        cp.wait_send()
    for cp in pending:
        cp.wait_send()
    for t in range(1, n_io):
        g = lax.rem(a + n_io - t, n_io)
        pltpu.make_async_remote_copy(slots.at[t - 1], restart.at[g], xs.at[t], xr.at[t],
                                     device_id={"io": lax.rem(a + t, n_io)}, device_id_type=MESH).wait_recv()
        for k in range(chunks):
            part = pl.ds(k * step_l, step_l)
            pltpu.make_async_remote_copy(slots2.at[t - 1, :, part], partner.at[g, :, part], ys.at[t, k], yr.at[t, k],
                                         device_id={"io": lax.rem(a + t, n_io)}, device_id_type=MESH).wait_recv()
    for cp in outs:
        cp.wait()


def per_device(tracer, anchor, east_flow, north_flow, diffusivity, land_mask, block_dest):
    n_io = lax.axis_size("io")
    levels, rows, cols = tracer.shape
    cap = max(2, 3 * rows // (2 * n_io))
    chunks = 5
    tile = pltpu.VMEM((rows, levels, cols), F32)
    dma = pltpu.SemaphoreType.DMA
    return pl.pallas_call(
        functools.partial(kernel, cap, chunks),
        out_shape=(
            jax.ShapeDtypeStruct((levels, rows, cols), F32),
            jax.ShapeDtypeStruct((n_io, cap, levels, cols), F32),
            jax.ShapeDtypeStruct((n_io, cap, levels, cols), F32),
        ),
        in_specs=[pl.BlockSpec(memory_space=pl.ANY)] * 6 + [pl.BlockSpec(memory_space=pltpu.SMEM)],
        out_specs=(
            pl.BlockSpec(memory_space=pl.ANY),
            pl.BlockSpec(memory_space=pltpu.VMEM),
            pl.BlockSpec(memory_space=pltpu.VMEM),
        ),
        scratch_shapes=[tile] * 8 + [pltpu.VMEM((rows, cols), jnp.int32), pltpu.VMEM((rows, cols), F32)]
        + [pltpu.VMEM((2, levels, cols), F32)] * 4
        + [pltpu.VMEM((3, levels, cols), F32)] * 4
        + [pltpu.VMEM((rows + 1, levels, cols), F32)]
        + [pltpu.VMEM((max(n_io - 1, 1), cap, levels, cols), F32)] * 2
        + [pltpu.VMEM((8, cols), jnp.int32)] * 2
        + [pltpu.SMEM((8, cols), jnp.int32)] * 2
        + [dma((6, rows)), dma((2,)), dma((2, 4)), dma((2, 4)), dma((chunks + 1,)), dma((chunks + 1,)),
           dma((n_io,)), dma((n_io,)), dma((n_io, chunks)), dma((n_io, chunks))]
        + [pltpu.VMEM((rows + 1, levels // chunks, cols), F32)] * chunks,
        compiler_params=pltpu.CompilerParams(collective_id=0, has_side_effects=True, vmem_limit_bytes=48 * 1024 * 1024),
        name="tracer_restart",
    )(tracer, anchor, east_flow, north_flow, diffusivity, land_mask, block_dest.reshape(rows))


def solution(mesh):
    placed = (
        P(None, "io", "comp"),
        P(None, "io", "comp"),
        P(None, "io", "comp"),
        P(None, "io", "comp"),
        P(None, "io", "comp"),
        P("io", "comp"),
        P("comp", "io", None),
    )
    return jax.shard_map(
        per_device,
        mesh=mesh,
        in_specs=placed,
        out_specs=(P(None, "io", "comp"), P("io", None, None, "comp"), P("io", None, None, "comp")),
        check_vma=False,
    )
```

```python
import functools
import jax
import jax.numpy as jnp
from jax import lax
from jax.experimental import pallas as pl
from jax.experimental.pallas import tpu as pltpu
from jax.sharding import PartitionSpec as P

MESH = pl.DeviceIdType.MESH
F32 = jnp.float32
BF16 = jnp.bfloat16


def kernel(cap, chunks, tracer, anchor, eflow, nflow, diff, mask, dest,
           out, restart, partner,
           f0, anc, ae, an, dd, be, bn, f1, mi, mf,
           east_s, west_s, east_r, west_r, north_s, south_s, north_r, south_r,
           packed, slots, slots2, table_v, table_p, table_s, table_ps,
           load_sem, table_sem, hs, hr, ps, pr, xs, xr, ys, yr, *got):
    n_comp, n_io = lax.axis_size("comp"), lax.axis_size("io")
    c, a = lax.axis_index("comp"), lax.axis_index("io")
    levels, rows, cols = tracer.shape
    east, west = lax.rem(c + 1, n_comp), lax.rem(c + n_comp - 1, n_comp)
    mate = lax.rem(c + n_comp // 2, n_comp)
    has_north, has_south = a < n_io - 1, a > 0

    zero = jnp.zeros((levels, cols), F32)
    for ref in (north_r, south_r):
        for k in range(3):
            ref[k] = zero

    barrier = pltpu.get_barrier_semaphore()
    for other in (east, west, mate):
        pl.semaphore_signal(barrier, inc=1, device_id={"comp": other}, device_id_type=MESH)
    for t in range(1, n_io):
        pl.semaphore_signal(barrier, inc=1, device_id={"io": lax.rem(a + t, n_io)}, device_id_type=MESH)

    loads = []
    mask_load = pltpu.make_async_copy(mask, mi, load_sem.at[5, 0])
    mask_load.start()
    for k, (src, dst) in enumerate(((tracer, f0), (eflow, ae), (nflow, an), (diff, dd), (anchor, anc))):
        for r in range(rows):
            cp = pltpu.make_async_copy(src.at[:, r, :], dst.at[r], load_sem.at[k, r])
            cp.start()
            loads.append(cp)

    lane = lax.broadcasted_iota(jnp.int32, (levels, cols), 1)
    packed[rows] = zero
    for ref in got:
        ref[rows] = zero[:levels // chunks]

    mask_load.wait()
    mf[...] = mi[...].astype(F32)
    m = mf[...]
    mb = m.astype(BF16)
    qi = lax.broadcasted_iota(jnp.int32, (cols, cols), 0)
    qj = lax.broadcasted_iota(jnp.int32, (cols, cols), 1)
    ki = lax.broadcasted_iota(jnp.int32, (rows, rows), 0)
    kj = lax.broadcasted_iota(jnp.int32, (rows, rows), 1)
    upto = jnp.where(qi <= qj, 1.0, 0.0).astype(BF16)
    before = jnp.where(kj < ki, 1.0, 0.0).astype(BF16)
    cum = jnp.dot(mb, upto, preferred_element_type=F32)
    tot = jnp.dot(mb, jnp.ones((cols, cols), BF16), preferred_element_type=F32)
    start = jnp.dot(before, tot.astype(BF16), preferred_element_type=F32)
    place = (start + cum - 1.0).astype(jnp.int32)
    place = jnp.where(m > 0.5, place & (cols - 1), -1)
    full_before = jnp.maximum(jnp.ceil(start * (1.0 / cols)) - 1.0, 0.0)
    full_after = jnp.maximum(jnp.ceil((start + tot) * (1.0 / cols)) - 1.0, 0.0)
    fill = start - full_before * cols
    over = full_after > full_before
    kk = lax.broadcasted_iota(jnp.int32, (rows, cols), 0)
    qq = lax.broadcasted_iota(jnp.int32, (rows, cols), 1)
    dvec = jnp.zeros((rows, cols), jnp.int32)
    for k in range(rows):
        dvec = jnp.where(kk == k, dest[k], dvec)
    group = jnp.zeros((rows, cols), jnp.int32)
    for g in range(1, n_io + 1):
        group = group + jnp.where(qq >= g * cap, 1, 0)
    slot = qq - group * cap
    hit = jnp.where(dvec == group, 1.0, 0.0)
    earlier = jnp.dot(before, hit.astype(BF16), preferred_element_type=F32)
    chosen = (dvec == group) & (earlier == slot.astype(F32))
    kq = jnp.min(jnp.where(chosen, kk, 1000).astype(F32), axis=0, keepdims=True)
    where_at = jnp.sum(jnp.where(full_after <= kq, 1.0, 0.0), axis=0, keepdims=True) - 1.0
    where_at = where_at + jnp.where(kq > full_after[rows - 1:rows], 1.0, 0.0)
    table_v[...] = jnp.broadcast_to(where_at.astype(jnp.int32), table_v.shape)
    table_load = pltpu.make_async_copy(table_v, table_s, table_sem.at[0])
    table_load.start()

    for cp in loads[:4 * rows]:
        cp.wait()

    for r in range(rows):
        mr = m[r:r + 1]
        u, v, d = ae[r], an[r], dd[r]
        ae[r] = mr * (jnp.maximum(u, 0.0) + d)
        be[r] = mr * (jnp.minimum(u, 0.0) - d)
        an[r] = mr * (jnp.maximum(v, 0.0) + d)
        bn[r] = mr * (jnp.minimum(v, 0.0) - d)

    last = cols - 1
    acc_e, acc_w = zero, zero
    for r in range(rows):
        acc_e = jnp.where(lane == r, (ae[r] * f0[r])[:, last:], acc_e)
        acc_e = jnp.where(lane == rows + r, be[r][:, last:], acc_e)
        acc_w = jnp.where(lane == r, f0[r][:, :1], acc_w)
        acc_w = jnp.where(lane == rows + r, jnp.broadcast_to(m[r:r + 1, :1], (levels, 1)), acc_w)
    east_s[0] = acc_e
    west_s[0] = acc_w
    north_s[0] = an[rows - 1] * f0[rows - 1]
    north_s[1] = bn[rows - 1]
    south_s[0] = f0[0]
    south_s[1] = jnp.broadcast_to(m[0:1], (levels, cols))

    pl.semaphore_wait(barrier, 3 + n_io - 1)

    def halo(step):
        where = slice(0, 2) if step == 0 else slice(2, 3)
        sel = pl.ds(where.start, where.stop - where.start)
        moves = [
            pltpu.make_async_remote_copy(east_s.at[step], east_r.at[step], hs.at[step, 0], hr.at[step, 0],
                                         device_id={"comp": east}, device_id_type=MESH),
            pltpu.make_async_remote_copy(west_s.at[step], west_r.at[step], hs.at[step, 1], hr.at[step, 1],
                                         device_id={"comp": west}, device_id_type=MESH),
        ]
        up = pltpu.make_async_remote_copy(north_s.at[sel], north_r.at[sel], hs.at[step, 2], hr.at[step, 2],
                                          device_id={"io": jnp.minimum(a + 1, n_io - 1)}, device_id_type=MESH)
        down = pltpu.make_async_remote_copy(south_s.at[sel], south_r.at[sel], hs.at[step, 3], hr.at[step, 3],
                                            device_id={"io": jnp.maximum(a - 1, 0)}, device_id_type=MESH)
        return moves, up, down

    def send_halo(step):
        moves, up, down = halo(step)
        for mv in moves:
            mv.start()
        pl.when(has_north)(up.start)
        pl.when(has_south)(down.start)

    def wait_halo(step):
        moves, up, down = halo(step)
        for mv in moves:
            mv.wait()

        @pl.when(has_north)
        def _():
            up.wait_send()
            down.wait_recv()

        @pl.when(has_south)
        def _():
            down.wait_send()
            up.wait_recv()

    send_halo(0)
    table_move = pltpu.make_async_remote_copy(table_v, table_p, ps.at[chunks], pr.at[chunks],
                                              device_id={"comp": mate}, device_id_type=MESH)
    table_move.start()
    wait_halo(0)

    west_0 = west_r[0]
    for r in range(rows):
        me = jnp.where(lane == last, west_0[:, rows + r:rows + r + 1], pltpu.roll(jnp.broadcast_to(m[r:r + 1], (levels, cols)), last, 1))
        ae[r] = ae[r] * me
        be[r] = be[r] * me
        mn = m[r + 1:r + 2] if r < rows - 1 else south_r[1]
        an[r] = an[r] * mn
        bn[r] = bn[r] * mn

    def row_of(step, src, r, fn_below):
        f = src[r]
        e_r, w_r = east_r[step], west_r[step]
        fe = jnp.where(lane == last, w_r[:, r:r + 1], pltpu.roll(f, last, 1))
        flux = ae[r] * f + be[r] * fe
        edge = m[r:r + 1] * (e_r[:, r:r + 1] + east_r[0][:, rows + r:rows + r + 1] * f)
        flux_w = jnp.where(lane == 0, edge, pltpu.roll(flux, 1, 1))
        fn = src[r + 1] if r < rows - 1 else south_r[0 if step == 0 else 2]
        flux_n = an[r] * f + bn[r] * fn
        return f - (flux - flux_w) - (flux_n - fn_below), flux_n

    flux_n = m[0:1] * (north_r[0] + north_r[1] * f0[0])
    acc_e, acc_w = zero, zero
    for r in range(rows):
        new, flux_n = row_of(0, f0, r, flux_n)
        f1[r] = new
        acc_e = jnp.where(lane == r, (ae[r] * new)[:, last:], acc_e)
        acc_w = jnp.where(lane == r, new[:, :1], acc_w)
        if r == 0:
            south_s[2] = new
        if r == rows - 1:
            north_s[2] = an[r] * new
    east_s[1] = acc_e
    west_s[1] = acc_w
    send_halo(1)
    for cp in loads[4 * rows:]:
        cp.wait()
    wait_halo(1)

    flux_n = m[0:1] * (north_r[2] + north_r[1] * f1[0])
    sub = lax.broadcasted_iota(jnp.int32, (cols, cols), 0)
    acc = zero
    outs = []
    for r in range(rows):
        new, flux_n = row_of(1, f1, r, flux_n)
        f0[r] = new
        cp = pltpu.make_async_copy(f0.at[r], out.at[:, r, :], load_sem.at[0, r])
        cp.start()
        outs.append(cp)
        delta = new - anc[r]
        hi = delta.astype(BF16).astype(F32)
        mid = (delta - hi).astype(BF16).astype(F32)
        low = delta - hi - mid
        parts = jnp.concatenate([hi, mid, low], axis=0).astype(BF16)
        pick = jnp.where(sub == place[r:r + 1], 1.0, 0.0).astype(BF16)
        got_r = lax.dot_general(parts, pick, (((1,), (1,)), ((), ())), preferred_element_type=F32)
        row = got_r[:levels] + got_r[levels:2 * levels] + got_r[2 * levels:]
        lanef = lane.astype(F32)
        begins = fill[r:r + 1]
        now = acc + jnp.where(lanef >= begins, row, 0.0)
        if r > 0:
            packed[r - 1] = now
        crossed = jnp.broadcast_to(jnp.where(over[r:r + 1], 1.0, 0.0), (levels, cols)) > 0.5
        acc = jnp.where(crossed, jnp.where(lanef < begins, row, 0.0), now)
    packed[rows - 1] = acc

    step_l = levels // chunks
    to_mate = []
    for k in range(chunks):
        part = pl.ds(k * step_l, step_l)
        cp = pltpu.make_async_remote_copy(packed.at[pl.ds(0, rows), part], got[k].at[pl.ds(0, rows)], ps.at[k], pr.at[k],
                                          device_id={"comp": mate}, device_id_type=MESH)
        cp.start()
        to_mate.append(cp)

    table_load.wait()
    pending = []
    for t in range(1, n_io):
        g = lax.rem(a + t, n_io)
        for s in range(cap):
            slots[t - 1, s] = packed[jnp.clip(table_s[0, g * cap + s], 0, rows)]
        cp = pltpu.make_async_remote_copy(slots.at[t - 1], restart.at[a], xs.at[t], xr.at[t],
                                          device_id={"io": g}, device_id_type=MESH)
        cp.start()
        pending.append(cp)
    for s in range(cap):
        slots[n_io - 1, s] = packed[jnp.clip(table_s[0, a * cap + s], 0, rows)]

    cp = pltpu.make_async_copy(slots.at[n_io - 1], restart.at[a], load_sem.at[1, 0])
    cp.start()
    outs.append(cp)

    table_move.wait()
    table_load = pltpu.make_async_copy(table_p, table_ps, table_sem.at[1])
    table_load.start()
    table_load.wait()
    for k in range(chunks):
        part = pl.ds(k * step_l, step_l)
        to_mate[k].wait_recv()
        for t in range(1, n_io):
            g = lax.rem(a + t, n_io)
            for s in range(cap):
                slots2[t - 1, s, part] = got[k][jnp.clip(table_ps[0, g * cap + s], 0, rows)]
            cp = pltpu.make_async_remote_copy(slots2.at[t - 1, :, part], partner.at[a, :, part], ys.at[t, k], yr.at[t, k],
                                              device_id={"io": g}, device_id_type=MESH)
            cp.start()
            pending.append(cp)
        for s in range(cap):
            slots2[n_io - 1, s, part] = got[k][jnp.clip(table_ps[0, a * cap + s], 0, rows)]
        cp = pltpu.make_async_copy(slots2.at[n_io - 1, :, part], partner.at[a, :, part], load_sem.at[2, k])
        cp.start()
        outs.append(cp)
    for cp in to_mate:
        cp.wait_send()
    for cp in pending:
        cp.wait_send()
    for t in range(1, n_io):
        g = lax.rem(a + n_io - t, n_io)
        pltpu.make_async_remote_copy(slots.at[t - 1], restart.at[g], xs.at[t], xr.at[t],
                                     device_id={"io": lax.rem(a + t, n_io)}, device_id_type=MESH).wait_recv()
        for k in range(chunks):
            part = pl.ds(k * step_l, step_l)
            pltpu.make_async_remote_copy(slots2.at[t - 1, :, part], partner.at[g, :, part], ys.at[t, k], yr.at[t, k],
                                         device_id={"io": lax.rem(a + t, n_io)}, device_id_type=MESH).wait_recv()
    for cp in outs:
        cp.wait()


def per_device(tracer, anchor, east_flow, north_flow, diffusivity, land_mask, block_dest):
    n_io = lax.axis_size("io")
    levels, rows, cols = tracer.shape
    cap = max(2, 3 * rows // (2 * n_io))
    chunks = 5
    tile = pltpu.VMEM((rows, levels, cols), F32)
    dma = pltpu.SemaphoreType.DMA
    return pl.pallas_call(
        functools.partial(kernel, cap, chunks),
        out_shape=(
            jax.ShapeDtypeStruct((levels, rows, cols), F32),
            jax.ShapeDtypeStruct((n_io, cap, levels, cols), F32),
            jax.ShapeDtypeStruct((n_io, cap, levels, cols), F32),
        ),
        in_specs=[pl.BlockSpec(memory_space=pl.ANY)] * 6 + [pl.BlockSpec(memory_space=pltpu.SMEM)],
        out_specs=(
            pl.BlockSpec(memory_space=pl.ANY),
            pl.BlockSpec(memory_space=pl.ANY),
            pl.BlockSpec(memory_space=pl.ANY),
        ),
        scratch_shapes=[tile] * 8 + [pltpu.VMEM((rows, cols), jnp.int32), pltpu.VMEM((rows, cols), F32)]
        + [pltpu.VMEM((2, levels, cols), F32)] * 4
        + [pltpu.VMEM((3, levels, cols), F32)] * 4
        + [pltpu.VMEM((rows + 1, levels, cols), F32)]
        + [pltpu.VMEM((n_io, cap, levels, cols), F32)] * 2
        + [pltpu.VMEM((8, cols), jnp.int32)] * 2
        + [pltpu.SMEM((8, cols), jnp.int32)] * 2
        + [dma((6, rows)), dma((2,)), dma((2, 4)), dma((2, 4)), dma((chunks + 1,)), dma((chunks + 1,)),
           dma((n_io,)), dma((n_io,)), dma((n_io, chunks)), dma((n_io, chunks))]
        + [pltpu.VMEM((rows + 1, levels // chunks, cols), F32)] * chunks,
        compiler_params=pltpu.CompilerParams(collective_id=0, has_side_effects=True),
        name="tracer_restart",
    )(tracer, anchor, east_flow, north_flow, diffusivity, land_mask, block_dest.reshape(rows))


def solution(mesh):
    placed = (
        P(None, "io", "comp"),
        P(None, "io", "comp"),
        P(None, "io", "comp"),
        P(None, "io", "comp"),
        P(None, "io", "comp"),
        P("io", "comp"),
        P("comp", "io", None),
    )
    return jax.shard_map(
        per_device,
        mesh=mesh,
        in_specs=placed,
        out_specs=(P(None, "io", "comp"), P("io", None, None, "comp"), P("io", None, None, "comp")),
        check_vma=False,
    )
```

```python
import functools
import jax
import jax.numpy as jnp
from jax import lax
from jax.experimental import pallas as pl
from jax.experimental.pallas import tpu as pltpu
from jax.sharding import PartitionSpec as P

MESH = pl.DeviceIdType.MESH
F32 = jnp.float32
BF16 = jnp.bfloat16


def kernel(cap, chunks, tracer, anchor, eflow, nflow, diff, mask, dest,
           out, restart, partner,
           f0, anc, ae, an, dd, be, bn, f1, mi, mf,
           east_s, west_s, east_r, west_r, north_s, south_s, north_r, south_r,
           packed, early, bulk_r, edges, edges_r, picks, mfp, slots, slots2, table_v, table_p, table_s, table_ps,
           load_sem, table_sem, hs, hr, ps, pr, xs, xr, ys, yr, *got):
    n_comp, n_io = lax.axis_size("comp"), lax.axis_size("io")
    c, a = lax.axis_index("comp"), lax.axis_index("io")
    levels, rows, cols = tracer.shape
    east, west = lax.rem(c + 1, n_comp), lax.rem(c + n_comp - 1, n_comp)
    mate = lax.rem(c + n_comp // 2, n_comp)
    has_north, has_south = a < n_io - 1, a > 0
    first = 4

    zero = jnp.zeros((levels, cols), F32)
    for ref in (north_r, south_r):
        for k in range(3):
            ref[k] = zero

    barrier = pltpu.get_barrier_semaphore()
    for other in (east, west, mate):
        pl.semaphore_signal(barrier, inc=1, device_id={"comp": other}, device_id_type=MESH)
    for t in range(1, n_io):
        pl.semaphore_signal(barrier, inc=1, device_id={"io": lax.rem(a + t, n_io)}, device_id_type=MESH)

    loads = []
    mask_load = pltpu.make_async_copy(mask, mi, load_sem.at[5, 0])
    mask_load.start()
    for k, (src, dst) in enumerate(((tracer, f0), (eflow, ae), (nflow, an), (diff, dd), (anchor, anc))):
        for r in range(rows):
            cp = pltpu.make_async_copy(src.at[:, r, :], dst.at[r], load_sem.at[k, r])
            cp.start()
            loads.append(cp)

    lane = lax.broadcasted_iota(jnp.int32, (levels, cols), 1)
    packed[rows] = zero
    for ref in got:
        ref[rows] = zero[:levels // chunks]

    mask_load.wait()
    mf[...] = mi[...].astype(F32)
    m = mf[...]
    qi = lax.broadcasted_iota(jnp.int32, (cols, cols), 0)
    qj = lax.broadcasted_iota(jnp.int32, (cols, cols), 1)
    ki = lax.broadcasted_iota(jnp.int32, (rows, rows), 0)
    kj = lax.broadcasted_iota(jnp.int32, (rows, rows), 1)
    upto = jnp.where(qi <= qj, 1.0, 0.0).astype(BF16)
    before = jnp.where(kj < ki, 1.0, 0.0).astype(BF16)

    def places(m):
        mb = m.astype(BF16)
        cum = jnp.dot(mb, upto, preferred_element_type=F32)
        tot = jnp.dot(mb, jnp.ones((cols, cols), BF16), preferred_element_type=F32)
        start = jnp.dot(before, tot.astype(BF16), preferred_element_type=F32)
        place = (start + cum - 1.0).astype(jnp.int32)
        place = jnp.where(m > 0.5, place & (cols - 1), -1)
        full_before = jnp.maximum(jnp.ceil(start * (1.0 / cols)) - 1.0, 0.0)
        full_after = jnp.maximum(jnp.ceil((start + tot) * (1.0 / cols)) - 1.0, 0.0)
        return place, start - full_before * cols, jnp.where(full_after > full_before, 1.0, 0.0), full_after

    place, fill, over, full_after = places(m)
    kk = lax.broadcasted_iota(jnp.int32, (rows, cols), 0)
    qq = lax.broadcasted_iota(jnp.int32, (rows, cols), 1)
    dvec = jnp.zeros((rows, cols), jnp.int32)
    for k in range(rows):
        dvec = jnp.where(kk == k, dest[k], dvec)
    group = jnp.zeros((rows, cols), jnp.int32)
    for g in range(1, n_io + 1):
        group = group + jnp.where(qq >= g * cap, 1, 0)
    slot = qq - group * cap
    hit = jnp.where(dvec == group, 1.0, 0.0)
    earlier = jnp.dot(before, hit.astype(BF16), preferred_element_type=F32)
    chosen = (dvec == group) & (earlier == slot.astype(F32))
    kq = jnp.min(jnp.where(chosen, kk, 1000).astype(F32), axis=0, keepdims=True)
    where_at = jnp.sum(jnp.where(full_after <= kq, 1.0, 0.0), axis=0, keepdims=True) - 1.0
    where_at = where_at + jnp.where(kq > full_after[rows - 1:rows], 1.0, 0.0)
    table_v[...] = jnp.broadcast_to(where_at.astype(jnp.int32), table_v.shape)
    table_load = pltpu.make_async_copy(table_v, table_s, table_sem.at[0])
    table_load.start()

    for cp in loads:
        cp.wait()

    for r in range(rows):
        mr = m[r:r + 1]
        u, v, d = ae[r], an[r], dd[r]
        ae[r] = mr * (jnp.maximum(u, 0.0) + d)
        be[r] = mr * (jnp.minimum(u, 0.0) - d)
        an[r] = mr * (jnp.maximum(v, 0.0) + d)
        bn[r] = mr * (jnp.minimum(v, 0.0) - d)

    last = cols - 1
    acc_e, acc_w = zero, zero
    for r in range(rows):
        acc_e = jnp.where(lane == r, (ae[r] * f0[r])[:, last:], acc_e)
        acc_e = jnp.where(lane == rows + r, be[r][:, last:], acc_e)
        acc_w = jnp.where(lane == r, f0[r][:, :1], acc_w)
        acc_w = jnp.where(lane == rows + r, jnp.broadcast_to(m[r:r + 1, :1], (levels, 1)), acc_w)
    east_s[0] = acc_e
    west_s[0] = acc_w
    north_s[0] = an[rows - 1] * f0[rows - 1]
    north_s[1] = bn[rows - 1]
    south_s[0] = f0[0]
    south_s[1] = jnp.broadcast_to(m[0:1], (levels, cols))

    pl.semaphore_wait(barrier, 3 + n_io - 1)

    def halo(step):
        where = slice(0, 2) if step == 0 else slice(2, 3)
        sel = pl.ds(where.start, where.stop - where.start)
        moves = [
            pltpu.make_async_remote_copy(east_s.at[step], east_r.at[step], hs.at[step, 0], hr.at[step, 0],
                                         device_id={"comp": east}, device_id_type=MESH),
            pltpu.make_async_remote_copy(west_s.at[step], west_r.at[step], hs.at[step, 1], hr.at[step, 1],
                                         device_id={"comp": west}, device_id_type=MESH),
        ]
        up = pltpu.make_async_remote_copy(north_s.at[sel], north_r.at[sel], hs.at[step, 2], hr.at[step, 2],
                                          device_id={"io": jnp.minimum(a + 1, n_io - 1)}, device_id_type=MESH)
        down = pltpu.make_async_remote_copy(south_s.at[sel], south_r.at[sel], hs.at[step, 3], hr.at[step, 3],
                                            device_id={"io": jnp.maximum(a - 1, 0)}, device_id_type=MESH)
        return moves, up, down

    def send_halo(step):
        moves, up, down = halo(step)
        for mv in moves:
            mv.start()
        pl.when(has_north)(up.start)
        pl.when(has_south)(down.start)

    def wait_halo(step):
        moves, up, down = halo(step)
        for mv in moves:
            mv.wait()

        @pl.when(has_north)
        def _():
            up.wait_send()
            down.wait_recv()

        @pl.when(has_south)
        def _():
            down.wait_send()
            up.wait_recv()

    send_halo(0)
    table_move = pltpu.make_async_remote_copy(table_v, table_p, ps.at[chunks], pr.at[chunks],
                                              device_id={"comp": mate}, device_id_type=MESH)
    table_move.start()
    mask_move = pltpu.make_async_remote_copy(mf, mfp, ps.at[chunks + 1], pr.at[chunks + 1],
                                             device_id={"comp": mate}, device_id_type=MESH)
    mask_move.start()

    for r in range(rows):
        me = jnp.where(lane == last, 1.0, pltpu.roll(jnp.broadcast_to(m[r:r + 1], (levels, cols)), last, 1))
        ae[r] = ae[r] * me
        be[r] = be[r] * me
        if r < rows - 1:
            an[r] = an[r] * m[r + 1:r + 2]
            bn[r] = bn[r] * m[r + 1:r + 2]

    def inner(src, r):
        f = src[r]
        flux = ae[r] * f + be[r] * pltpu.roll(f, last, 1)
        return f - (flux - pltpu.roll(flux, 1, 1))

    def north_flux(src, r):
        return an[r] * src[r] + bn[r] * src[r + 1]

    below = north_flux(f0, 0)
    for r in range(1, rows - 1):
        above = north_flux(f0, r)
        f1[r] = inner(f0, r) - (above - below)
        below = above
    below = north_flux(f1, 1)
    for r in range(2, rows - 2):
        above = north_flux(f1, r)
        early[r - 2] = inner(f1, r) - (above - below) - anc[r]
        below = above
    cuts = ((0, first), (first, rows - 4 - first))
    bulk = [pltpu.make_async_remote_copy(early.at[pl.ds(at, many)], bulk_r.at[pl.ds(at, many)], ps.at[chunks + 2 + k],
                                         pr.at[chunks + 2 + k], device_id={"comp": mate}, device_id_type=MESH)
            for k, (at, many) in enumerate(cuts)]
    bulk[0].start()

    wait_halo(0)
    west_0 = west_r[0]
    for r in range(rows):
        me = jnp.where(lane == last, west_0[:, rows + r:rows + r + 1], 1.0)
        ae[r] = ae[r] * me
        be[r] = be[r] * me
    an[rows - 1] = an[rows - 1] * south_r[1]
    bn[rows - 1] = bn[rows - 1] * south_r[1]

    def row_of(step, src, r, fn_below):
        f = src[r]
        e_r, w_r = east_r[step], west_r[step]
        fe = jnp.where(lane == last, w_r[:, r:r + 1], pltpu.roll(f, last, 1))
        flux = ae[r] * f + be[r] * fe
        edge = m[r:r + 1] * (e_r[:, r:r + 1] + east_r[0][:, rows + r:rows + r + 1] * f)
        flux_w = jnp.where(lane == 0, edge, pltpu.roll(flux, 1, 1))
        fn = src[r + 1] if r < rows - 1 else south_r[0 if step == 0 else 2]
        flux_n = an[r] * f + bn[r] * fn
        return f - (flux - flux_w) - (flux_n - fn_below), flux_n

    flux_n = m[0:1] * (north_r[0] + north_r[1] * f0[0])
    acc_e, acc_w = zero, zero
    for r in range(rows):
        new, flux_n = row_of(0, f0, r, flux_n)
        f1[r] = new
        acc_e = jnp.where(lane == r, (ae[r] * new)[:, last:], acc_e)
        acc_w = jnp.where(lane == r, new[:, :1], acc_w)
        if r == 0:
            south_s[2] = new
        if r == rows - 1:
            north_s[2] = an[r] * new
    east_s[1] = acc_e
    west_s[1] = acc_w
    send_halo(1)
    bulk[1].start()
    wait_halo(1)

    flux_n = m[0:1] * (north_r[2] + north_r[1] * f1[0])
    outs = []
    acc_f = zero
    edge_rows = (0, 1, rows - 2, rows - 1)
    edge_cols = (0, 1, cols - 2, cols - 1)
    for r in range(rows):
        new, flux_n = row_of(1, f1, r, flux_n)
        f0[r] = new
        cp = pltpu.make_async_copy(f0.at[r], out.at[:, r, :], load_sem.at[0, r])
        cp.start()
        outs.append(cp)
        delta = new - anc[r]
        anc[r] = delta
        if r in edge_rows:
            edges[edge_rows.index(r)] = delta
        else:
            for k, col in enumerate(edge_cols):
                acc_f = jnp.where(lane == k * rows + r, delta[:, col:col + 1], acc_f)
    edges[4] = acc_f
    step_l = levels // chunks
    to_mate = []
    for k in range(chunks):
        part = pl.ds(k * step_l, step_l)
        cp = pltpu.make_async_remote_copy(edges.at[:, part], edges_r.at[:, part], ps.at[k], pr.at[k],
                                          device_id={"comp": mate}, device_id_type=MESH)
        cp.start()
        to_mate.append(cp)

    sub = lax.broadcasted_iota(jnp.int32, (cols, cols), 0)

    def one_hot(place, r):
        return jnp.where(sub == place[r:r + 1], 1.0, 0.0).astype(BF16)

    def compact(delta_of, pick_of, fill, over, store):
        acc = None
        for r in range(rows):
            delta = delta_of(r)
            n = delta.shape[0]
            hi = delta.astype(BF16).astype(F32)
            mid = (delta - hi).astype(BF16).astype(F32)
            low = delta - hi - mid
            parts = jnp.concatenate([hi, mid, low], axis=0).astype(BF16)
            moved = lax.dot_general(parts, pick_of(r), (((1,), (1,)), ((), ())), preferred_element_type=F32)
            row = moved[:n] + moved[n:2 * n] + moved[2 * n:]
            if r == 0:
                acc = row
                continue
            starts = lax.broadcasted_iota(jnp.int32, (n, cols), 1).astype(F32) >= fill[r:r + 1]
            now = acc + jnp.where(starts, row, 0.0)
            store(r - 1, now)
            crossed = jnp.broadcast_to(over[r:r + 1], (n, cols)) > 0.5
            acc = jnp.where(crossed, jnp.where(starts, 0.0, row), now)
        store(rows - 1, acc)

    def keep(r, block):
        packed[r] = block

    compact(lambda r: anc[r], lambda r: one_hot(place, r), fill, over, keep)

    table_load.wait()
    pending = []
    for t in range(1, n_io):
        g = lax.rem(a + t, n_io)
        for s in range(cap):
            slots[t - 1, s] = packed[jnp.clip(table_s[0, g * cap + s], 0, rows)]
        cp = pltpu.make_async_remote_copy(slots.at[t - 1], restart.at[a], xs.at[t], xr.at[t],
                                          device_id={"io": g}, device_id_type=MESH)
        cp.start()
        pending.append(cp)
    for s in range(cap):
        slots[n_io - 1, s] = packed[jnp.clip(table_s[0, a * cap + s], 0, rows)]

    cp = pltpu.make_async_copy(slots.at[n_io - 1], restart.at[a], load_sem.at[1, 0])
    cp.start()
    outs.append(cp)

    table_move.wait()
    table_load = pltpu.make_async_copy(table_p, table_ps, table_sem.at[1])
    table_load.start()
    mask_move.wait()
    place_p, fill_p, over_p, _ = places(mfp[...])
    for r in range(rows):
        picks[r] = one_hot(place_p, r)
    table_load.wait()
    for cp in bulk:
        cp.wait()
    lane_l = lax.broadcasted_iota(jnp.int32, (step_l, cols), 1)
    for k in range(chunks):
        part = pl.ds(k * step_l, step_l)
        to_mate[k].wait_recv()

        def delta_of(r):
            if r in edge_rows:
                return edges_r[edge_rows.index(r), part]
            delta, sides = bulk_r[r - 2, part], edges_r[4, part]
            for q, col in enumerate(edge_cols):
                delta = jnp.where(lane_l == col, sides[:, q * rows + r:q * rows + r + 1], delta)
            return delta

        def keep_p(r, block):
            got[k][r] = block

        compact(delta_of, lambda r: picks[r], fill_p, over_p, keep_p)
        for t in range(1, n_io):
            g = lax.rem(a + t, n_io)
            for s in range(cap):
                slots2[t - 1, s, part] = got[k][jnp.clip(table_ps[0, g * cap + s], 0, rows)]
            cp = pltpu.make_async_remote_copy(slots2.at[t - 1, :, part], partner.at[a, :, part], ys.at[t, k], yr.at[t, k],
                                              device_id={"io": g}, device_id_type=MESH)
            cp.start()
            pending.append(cp)
        for s in range(cap):
            slots2[n_io - 1, s, part] = got[k][jnp.clip(table_ps[0, a * cap + s], 0, rows)]
        cp = pltpu.make_async_copy(slots2.at[n_io - 1, :, part], partner.at[a, :, part], load_sem.at[2, k])
        cp.start()
        outs.append(cp)
    for cp in to_mate:
        cp.wait_send()
    for cp in pending:
        cp.wait_send()
    for t in range(1, n_io):
        g = lax.rem(a + n_io - t, n_io)
        pltpu.make_async_remote_copy(slots.at[t - 1], restart.at[g], xs.at[t], xr.at[t],
                                     device_id={"io": lax.rem(a + t, n_io)}, device_id_type=MESH).wait_recv()
        for k in range(chunks):
            part = pl.ds(k * step_l, step_l)
            pltpu.make_async_remote_copy(slots2.at[t - 1, :, part], partner.at[g, :, part], ys.at[t, k], yr.at[t, k],
                                         device_id={"io": lax.rem(a + t, n_io)}, device_id_type=MESH).wait_recv()
    for cp in outs:
        cp.wait()


def per_device(tracer, anchor, east_flow, north_flow, diffusivity, land_mask, block_dest):
    n_io = lax.axis_size("io")
    levels, rows, cols = tracer.shape
    cap = max(2, 3 * rows // (2 * n_io))
    chunks = 5
    tile = pltpu.VMEM((rows, levels, cols), F32)
    dma = pltpu.SemaphoreType.DMA
    return pl.pallas_call(
        functools.partial(kernel, cap, chunks),
        out_shape=(
            jax.ShapeDtypeStruct((levels, rows, cols), F32),
            jax.ShapeDtypeStruct((n_io, cap, levels, cols), F32),
            jax.ShapeDtypeStruct((n_io, cap, levels, cols), F32),
        ),
        in_specs=[pl.BlockSpec(memory_space=pl.ANY)] * 6 + [pl.BlockSpec(memory_space=pltpu.SMEM)],
        out_specs=(
            pl.BlockSpec(memory_space=pl.ANY),
            pl.BlockSpec(memory_space=pl.ANY),
            pl.BlockSpec(memory_space=pl.ANY),
        ),
        scratch_shapes=[tile] * 8 + [pltpu.VMEM((rows, cols), jnp.int32), pltpu.VMEM((rows, cols), F32)]
        + [pltpu.VMEM((2, levels, cols), F32)] * 4
        + [pltpu.VMEM((3, levels, cols), F32)] * 4
        + [pltpu.VMEM((rows + 1, levels, cols), F32)]
        + [pltpu.VMEM((rows - 4, levels, cols), F32)] * 2
        + [pltpu.VMEM((5, levels, cols), F32)] * 2
        + [pltpu.VMEM((rows, cols, cols), BF16), pltpu.VMEM((rows, cols), F32)]
        + [pltpu.VMEM((n_io, cap, levels, cols), F32)] * 2
        + [pltpu.VMEM((8, cols), jnp.int32)] * 2
        + [pltpu.SMEM((8, cols), jnp.int32)] * 2
        + [dma((6, rows)), dma((2,)), dma((2, 4)), dma((2, 4)), dma((chunks + 4,)), dma((chunks + 4,)),
           dma((n_io,)), dma((n_io,)), dma((n_io, chunks)), dma((n_io, chunks))]
        + [pltpu.VMEM((rows + 1, levels // chunks, cols), F32)] * chunks,
        compiler_params=pltpu.CompilerParams(collective_id=0, has_side_effects=True),
        name="tracer_restart",
    )(tracer, anchor, east_flow, north_flow, diffusivity, land_mask, block_dest.reshape(rows))


def solution(mesh):
    placed = (
        P(None, "io", "comp"),
        P(None, "io", "comp"),
        P(None, "io", "comp"),
        P(None, "io", "comp"),
        P(None, "io", "comp"),
        P("io", "comp"),
        P("comp", "io", None),
    )
    return jax.shard_map(
        per_device,
        mesh=mesh,
        in_specs=placed,
        out_specs=(P(None, "io", "comp"), P("io", None, None, "comp"), P("io", None, None, "comp")),
        check_vma=False,
    )
```
